32 devices in a mesh: row: 8 (over y, x, core), col: 4 (over z).
Axes of the slice: x: 2, y: 2, z: 4, core: 2. Of those that a mesh axis runs over, the one named last changes fastest.
Arguments:
- inputs_act: bfloat16 [1024, 4096], P('row', 'col'), may hold values from -6 to 6
- out_grad: bfloat16 [1024, 4096], P('row', 'col'), may hold values from -6 to 6
- pre_act: bfloat16 [1024, 16384], P('col', 'row'), may hold values from -8 to 8
- w_first: bfloat16 [4096, 16384], P('col', 'row'), may hold values from -0.046875 to 0.046875
- w_second: bfloat16 [16384, 4096], P('row', 'col'), may hold values from -0.09375 to 0.09375
Outputs:
- grad_input: bfloat16 [1024, 4096], P('row', 'col')
- grad_first: float32 [4096, 16384], P('col', 'row')
- grad_second: float32 [16384, 4096], P('row', 'col')
The draws below stay inside these ranges and needn't reach their ends.
All inputs are finite; a program needn't handle non-finite values.
Results may differ from the reference program's by a relative error of at most 0.019.
Values may be sent and summed in bfloat16 or wider, within the bound.
A program may use at most 128 MiB of HBM per device.

```python
import math
import jax
import jax.numpy as jnp
from jax import lax

D = 4096
H = 16384
TOKENS = 1024
N_ROW = 8


def shard_levels(key, extent, cuts, low, largest):
    def one(dim, blocks):
        draws = jax.random.uniform(jax.random.fold_in(jax.random.fold_in(key, 6), dim), (blocks,), jnp.float32, low / len(cuts), largest / len(cuts))
        return jnp.repeat(jnp.exp(draws), extent[dim] // blocks).reshape((-1,) + (1,) * (len(extent) - dim - 1))

    level = one(*cuts[0])
    for cut in cuts[1:]:
        level = level * one(*cut)
    return level


def normal_values(rng, shape, spread, bound, pieces=(), held_as=jnp.bfloat16):
    array = jax.random.normal(rng, shape, jnp.float32) * spread
    if len(pieces) > 0:
        array = shard_levels(rng, shape, pieces, -0.22, 0.18) * array
    return jnp.clip(array, min=-bound, max=bound).astype(held_as)


def setup_inputs(seed: int = 0) -> dict:
    key_of = jax.random.split(jax.random.key(seed), 6)
    inputs_act = normal_values(key_of[0], (TOKENS, D), 1.0, 6.0, ((0, 8), (1, 4)))
    out_grad = normal_values(key_of[1], (TOKENS, D), 1.0, 6.0, ((0, 8), (1, 4)))
    pre_act = normal_values(key_of[2], (TOKENS, H), 1.5, 8.0, ((0, 4), (1, 8)))
    w_first = normal_values(key_of[3], (D, H), H ** -0.5, 0.046875, ((0, 4), (1, 8)))
    w_second = normal_values(key_of[4], (H, D), D ** -0.5, 0.09375, ((0, 8), (1, 4)))
    return dict(inputs_act=inputs_act, out_grad=out_grad, pre_act=pre_act, w_first=w_first, w_second=w_second)


gelu_coef = 0.044715

def gelu_pair(pre_float):
    inner_c = math.sqrt(2.0 / math.pi)
    inner = inner_c * (pre_float + gelu_coef * pre_float * pre_float * pre_float)
    tanh_val = jnp.tanh(inner)
    act = 0.5 * pre_float * (1.0 + tanh_val)
    slope = 0.5 * (1.0 + tanh_val) + 0.5 * pre_float * (1.0 - tanh_val * tanh_val) * inner_c * (1.0 + 3.0 * gelu_coef * pre_float * pre_float)
    return (act, slope)

def reference(inputs_act, out_grad, pre_act, w_first, w_second):
    act_float, slope = gelu_pair(pre_act.astype(jnp.float32))
    act = act_float.astype(jnp.bfloat16)
    grad_hidden = lax.dot_general(out_grad, w_second, (((1,), (1,)), ((), ())), preferred_element_type=jnp.float32)
    grad_pre = (grad_hidden * slope).astype(jnp.bfloat16)
    block_width = H // N_ROW

    def add_block(running, block_index):
        start = (block_index * block_width).astype(jnp.int32)
        grad_block = lax.dynamic_slice_in_dim(grad_pre, start, block_width, 1)
        weight_block = lax.dynamic_slice_in_dim(w_first, start, block_width, 1)
        partial_sum = lax.dot_general(grad_block, weight_block, (((1,), (1,)), ((), ())), preferred_element_type=jnp.float32)
        rounded = lax.optimization_barrier(partial_sum.astype(jnp.bfloat16))
        return (running + rounded.astype(jnp.float32), None)
    start_total = jnp.zeros((grad_pre.shape[0], w_first.shape[0]), jnp.float32)
    input_total, unused = lax.scan(add_block, start_total, jnp.arange(N_ROW, dtype=jnp.int32))
    grad_input = input_total.astype(jnp.bfloat16)
    factor = 1.0 / math.sqrt(TOKENS)
    grad_first = lax.dot_general(inputs_act, grad_pre, (((0,), (0,)), ((), ())), preferred_element_type=jnp.float32) * factor
    grad_second = lax.dot_general(act, out_grad, (((0,), (0,)), ((), ())), preferred_element_type=jnp.float32) * factor
    return (grad_input, grad_first, grad_second)
```

```python
import functools
import math

import jax
import jax.numpy as jnp
from jax import lax
from jax.experimental import pallas as pl
from jax.experimental.pallas import tpu as pltpu
from jax.sharding import PartitionSpec as P

gelu_coef = 0.044715
inner_c = math.sqrt(2.0 / math.pi)
SUB = 2
STRIP = 16
MESH = pl.DeviceIdType.MESH


def tanh_of(p):
    return jnp.tanh(inner_c * (p + gelu_coef * p * p * p))


def act_of(p):
    return 0.5 * p * (1.0 + tanh_of(p))


def slope_of(p):
    t = tanh_of(p)
    return 0.5 * (1.0 + t) + 0.5 * p * (1.0 - t * t) * inner_c * (1.0 + 3.0 * gelu_coef * p * p)


def contract_last(left, right):
    return lax.dot_general(
        left, right, (((1,), (1,)), ((), ())), preferred_element_type=jnp.float32
    )


def contract_first(left, right):
    return lax.dot_general(
        left, right, (((0,), (0,)), ((), ())), preferred_element_type=jnp.float32
    )


def strips(first, count, body):
    def one(i, carry):
        body(pl.ds(pl.multiple_of(first + i * STRIP, STRIP), STRIP))
        return carry

    lax.fori_loop(0, count // STRIP, one, 0)


def kernel(
    R, N,
    x_ref, dy_ref, pre_ref, w1_ref, w2_ref,
    gi_out, x_out, dy_out, act_out, gp_out,
    w1, w2, dy, hid, pre, gp, act, slope, rs, gi_send, gi_recv, acc,
    loc, out_sem, dy_s, dy_r, x_s, x_r, pr_s, pr_r, rs_s, rs_r, gp_s, gp_r, gi_s, gi_r,
):
    r = lax.axis_index("row")
    c = lax.axis_index("col")
    q = R // N
    Tr = dy_ref.shape[0]
    Tc, H = pre_ref.shape
    Dc = dy_ref.shape[1]
    part = Tc // SUB
    last = N - 1
    f32, bf16 = jnp.float32, jnp.bfloat16

    barrier = pltpu.get_barrier_semaphore()
    for k in range(1, R):
        pl.semaphore_signal(barrier, inc=1, device_id={"row": lax.rem(r + k, R)}, device_id_type=MESH)

    @pl.when(c > 0)
    def _():
        pl.semaphore_signal(barrier, inc=1, device_id={"col": c - 1}, device_id_type=MESH)

    @pl.when(c < last)
    def _():
        pl.semaphore_signal(barrier, inc=1, device_id={"col": c + 1}, device_id_type=MESH)

    local = [
        pltpu.make_async_copy(dy_ref, dy.at[r], loc.at[0]),
        pltpu.make_async_copy(pre_ref, pre.at[c], loc.at[1]),
        pltpu.make_async_copy(w2_ref, w2, loc.at[2]),
        pltpu.make_async_copy(w1_ref, w1, loc.at[3]),
        pltpu.make_async_copy(x_ref, x_out.at[r], loc.at[4]),
    ]
    for copy in local:
        copy.start()
    ends = jnp.where(c > 0, 1, 0) + jnp.where(c < last, 1, 0)
    pl.semaphore_wait(barrier, R - 1 + ends)

    def row_send(src, dst, k, send, recv):
        return pltpu.make_async_remote_copy(
            src_ref=src, dst_ref=dst.at[r], send_sem=send.at[k], recv_sem=recv.at[r],
            device_id={"row": lax.rem(r + k, R)}, device_id_type=MESH)

    def row_recv(src, dst, k, send, recv):
        p = lax.rem(r + k, R)
        return pltpu.make_async_remote_copy(
            src_ref=src, dst_ref=dst.at[p], send_sem=send.at[k], recv_sem=recv.at[p],
            device_id={"row": p}, device_id_type=MESH)

    def sends_to(side):
        return c + 1 if side == 0 else c - 1

    def ag_shard(side, k):
        return c - k if side == 0 else c + k

    def ag_sends(side, k):
        return (c < last) & (c >= k) if side == 0 else (c > 0) & (c + k <= last)

    def ag_gets(side, k):
        return c >= k + 1 if side == 0 else c + 1 + k <= last

    def ag_got(side, k):
        return c - 1 - k if side == 0 else c + 1 + k

    def ag_copy(buf, shard, rows, side, send, recv, src=None):
        place = buf.at[shard] if rows is None else buf.at[shard, rows]
        return pltpu.make_async_remote_copy(
            src_ref=place if src is None else src, dst_ref=place, send_sem=send, recv_sem=recv,
            device_id={"col": sends_to(side)}, device_id_type=MESH)

    def rs_shard(side, k):
        return last - k + c if side == 0 else k - last + c

    def rs_sends(side, k):
        return c <= k if side == 0 else last - c <= k

    def rs_copy(side, k, j):
        rows = pl.ds(j * part, part)
        return pltpu.make_async_remote_copy(
            src_ref=hid.at[rs_shard(side, k), rows], dst_ref=rs.at[side, k, rows],
            send_sem=rs_s.at[side, k, j], recv_sem=rs_r.at[side, k, j],
            device_id={"col": sends_to(side)}, device_id_type=MESH)

    def rs_arrived(side, k, j):
        rows = pl.ds(j * part, part)
        return pltpu.make_async_remote_copy(
            src_ref=hid.at[c, rows], dst_ref=rs.at[side, k, rows],
            send_sem=rs_s.at[side, k, j], recv_sem=rs_r.at[side, k, j],
            device_id={"col": sends_to(side)}, device_id_type=MESH)

    def pre_step(k):
        for side in range(2):
            @pl.when(ag_sends(side, k))
            def _():
                if k > 0:
                    ag_copy(pre, ag_shard(side, k), None, side, pr_s.at[side, k - 1],
                            pr_r.at[side, k - 1]).wait_recv()
                ag_copy(pre, ag_shard(side, k), None, side, pr_s.at[side, k], pr_r.at[side, k],
                        pre_ref if k == 0 else None).start()

    for k in range(1, R):
        row_send(dy_ref, dy, k, dy_s, dy_r).start()
    pre_step(0)

    local[1].wait()

    def slope_strip(rows):
        slope[rows, :] = slope_of(pre[c, rows, :].astype(f32))

    strips(0, Tc, slope_strip)

    local[0].wait()
    local[2].wait()
    for k in range(1, R):
        row_recv(dy_ref, dy, k, dy_s, dy_r).wait_recv()
    for k in range(1, R):
        row_send(x_ref, x_out, k, x_s, x_r).start()

    tile_h = min(512, H)

    def partial(s):
        def one(i, carry):
            cols = pl.ds(pl.multiple_of(i * tile_h, tile_h), tile_h)
            left = dy[q * s : q * s + q].reshape(Tc, Dc)
            hid[s, :, cols] = contract_last(left, w2[cols, :]).astype(bf16)
            return carry

        lax.fori_loop(0, H // tile_h, one, 0)

    order = []
    for i in range((N + 1) // 2):
        order += [last - i] + ([i] if i != last - i else [])
    for s in order:
        partial(s)
        if s == last:
            @pl.when(c == 0)
            def _():
                for j in range(SUB):
                    rs_copy(0, 0, j).start()
        if s == 0:
            @pl.when(c == last)
            def _():
                for j in range(SUB):
                    rs_copy(1, 0, j).start()
    dy_copy = pltpu.make_async_copy(dy, dy_out, out_sem.at[0])
    dy_copy.start()

    pre_step(1)
    for k in range(1, last):
        for j in range(SUB):
            for side in range(2):
                edge = c == 0 if side == 0 else c == last

                @pl.when(rs_sends(side, k) & jnp.logical_not(edge))
                def _():
                    rs_arrived(side, k - 1, j).wait_recv()
                    s = rs_shard(side, k)

                    def add(rows):
                        total = hid[s, rows, :].astype(f32) + rs[side, k - 1, rows, :].astype(f32)
                        hid[s, rows, :] = total.astype(bf16)

                    strips(j * part, part, add)

                @pl.when(rs_sends(side, k))
                def _():
                    @pl.when(rs_sends(side, k - 1))
                    def _():
                        rs_copy(side, k - 1, j).wait_send()

                    rs_copy(side, k, j).start()
        if k + 1 < last:
            pre_step(k + 1)

    for j in range(SUB):
        rows_j = pl.ds(j * part, part)

        def load(rows):
            acc[rows, :] = hid[c, rows, :].astype(f32)

        strips(j * part, part, load)
        for side in range(2):
            @pl.when(c > 0 if side == 0 else c < last)
            def _():
                rs_arrived(side, last - 1, j).wait_recv()

                def add(rows):
                    acc[rows, :] = acc[rows, :] + rs[side, last - 1, rows, :].astype(f32)

                strips(j * part, part, add)

        def scale(rows):
            gp[c, rows, :] = (acc[rows, :] * slope[rows, :]).astype(bf16)

        strips(j * part, part, scale)
        for side in range(2):
            @pl.when(ag_sends(side, 0))
            def _():
                ag_copy(gp, c, rows_j, side, gp_s.at[side, 0, j], gp_r.at[side, 0, j]).start()

    local[3].wait()
    tile_d = min(512, Dc)

    def gi_copy(s, i):
        to = q * s + i
        return pltpu.make_async_remote_copy(
            src_ref=gi_send.at[s, pl.ds(i * Tr, Tr)], dst_ref=gi_recv.at[r],
            send_sem=gi_s.at[to], recv_sem=gi_r.at[r], device_id={"row": to}, device_id_type=MESH)

    def use_block(s):
        pltpu.make_async_copy(gp.at[s], gp_out.at[s], out_sem.at[1 + s]).start()

        def one(i, carry):
            cols = pl.ds(pl.multiple_of(i * tile_d, tile_d), tile_d)
            gi_send[s, :, cols] = contract_last(gp[s], w1[cols, :]).astype(bf16)
            return carry

        lax.fori_loop(0, Dc // tile_d, one, 0)
        for i in range(q):
            to = q * s + i

            @pl.when(to != r)
            def _():
                gi_copy(s, i).start()

            @pl.when(to == r)
            def _():
                gi_recv[r] = gi_send[s, pl.ds(i * Tr, Tr), :]

    def act_block(s):
        def one(rows):
            act[s, rows, :] = act_of(pre[s, rows, :].astype(f32)).astype(bf16)

        strips(0, Tc, one)
        pltpu.make_async_copy(act.at[s], act_out.at[s], out_sem.at[1 + N + s]).start()

    use_block(c)
    act_block(c)

    for k in range(last):
        for j in range(SUB):
            rows_j = pl.ds(j * part, part)
            for side in range(2):
                @pl.when(ag_gets(side, k))
                def _():
                    s = ag_got(side, k)
                    ag_copy(gp, s, rows_j, side, gp_s.at[side, k, j], gp_r.at[side, k, j]).wait_recv()
                    if k + 1 < last:
                        @pl.when(ag_sends(side, k + 1))
                        def _():
                            ag_copy(gp, s, rows_j, side, gp_s.at[side, k + 1, j],
                                    gp_r.at[side, k + 1, j]).start()
        for side in range(2):
            @pl.when(ag_gets(side, k))
            def _():
                s = ag_got(side, k)
                use_block(s)
                forwarded = ag_sends(side, k + 1) if k + 1 < last else c < 0

                @pl.when(jnp.logical_not(forwarded))
                def _():
                    ag_copy(pre, s, None, side, pr_s.at[side, k], pr_r.at[side, k]).wait_recv()

                act_block(s)

    for k in range(1, R):
        row_recv(gi_send.at[0, pl.ds(0, Tr)], gi_recv, k, gi_s, gi_r).wait_recv()

    def total_strip(rows):
        total = gi_recv[0, rows, :].astype(f32)
        for p in range(1, R):
            total = total + gi_recv[p, rows, :].astype(f32)
        gi_out[rows, :] = total.astype(bf16)

    strips(0, Tr, total_strip)

    for k in range(1, R):
        row_send(dy_ref, dy, k, dy_s, dy_r).wait_send()
        row_send(x_ref, x_out, k, x_s, x_r).wait_send()
        row_recv(x_ref, x_out, k, x_s, x_r).wait_recv()
    for s in range(N):
        for i in range(q):
            @pl.when(q * s + i != r)
            def _():
                gi_copy(s, i).wait_send()
        pltpu.make_async_copy(gp.at[s], gp_out.at[s], out_sem.at[1 + s]).wait()
        pltpu.make_async_copy(act.at[s], act_out.at[s], out_sem.at[1 + N + s]).wait()
    for side in range(2):
        for k in range(last):
            @pl.when(ag_sends(side, k))
            def _():
                s = ag_shard(side, k)
                ag_copy(pre, s, None, side, pr_s.at[side, k], pr_r.at[side, k],
                        pre_ref if k == 0 else None).wait_send()
                for j in range(SUB):
                    ag_copy(gp, s, pl.ds(j * part, part), side, gp_s.at[side, k, j],
                            gp_r.at[side, k, j]).wait_send()

        @pl.when(rs_sends(side, last - 1))
        def _():
            for j in range(SUB):
                rs_copy(side, last - 1, j).wait_send()
    dy_copy.wait()
    local[4].wait()


def exchange(R, N, x, dy, pre, w1, w2):
    Tr, Dc = dy.shape
    Tc, H = pre.shape
    bf16 = jnp.bfloat16
    dma = pltpu.SemaphoreType.DMA
    hbm = pl.BlockSpec(memory_space=pl.ANY)
    return pl.pallas_call(
        functools.partial(kernel, R, N),
        out_shape=[
            jax.ShapeDtypeStruct((Tr, Dc), bf16),
            jax.ShapeDtypeStruct((R, Tr, Dc), bf16),
            jax.ShapeDtypeStruct((R, Tr, Dc), bf16),
            jax.ShapeDtypeStruct((N, Tc, H), bf16),
            jax.ShapeDtypeStruct((N, Tc, H), bf16),
        ],
        in_specs=[hbm] * 5,
        out_specs=[pl.BlockSpec(memory_space=pltpu.VMEM)] + [hbm] * 4,
        scratch_shapes=[
            pltpu.VMEM(w1.shape, bf16),
            pltpu.VMEM(w2.shape, bf16),
            pltpu.VMEM((R, Tr, Dc), bf16),
            pltpu.VMEM((N, Tc, H), bf16),
            pltpu.VMEM((N, Tc, H), bf16),
            pltpu.VMEM((N, Tc, H), bf16),
            pltpu.VMEM((N, Tc, H), bf16),
            pltpu.VMEM((Tc, H), jnp.float32),
            pltpu.VMEM((2, N - 1, Tc, H), bf16),
            pltpu.VMEM((N, Tc, Dc), bf16),
            pltpu.VMEM((R, Tr, Dc), bf16),
            pltpu.VMEM((Tc, H), jnp.float32),
            dma((5,)),
            dma((1 + 2 * N,)),
            dma((R,)), dma((R,)), dma((R,)), dma((R,)),
            dma((2, N - 1)), dma((2, N - 1)),
            dma((2, N - 1, SUB)), dma((2, N - 1, SUB)),
            dma((2, N - 1, SUB)), dma((2, N - 1, SUB)),
            dma((R,)), dma((R,)),
        ],
        compiler_params=pltpu.CompilerParams(
            collective_id=0, has_side_effects=True, vmem_limit_bytes=56 * 2**20
        ),
    )(x, dy, pre, w1, w2)


def on_device(R, N, inputs_act, out_grad, pre_act, w_first, w_second):
    total_tokens = pre_act.shape[0] * N
    factor = 1.0 / math.sqrt(total_tokens)
    grad_input, x, dy, act, gp = exchange(R, N, inputs_act, out_grad, pre_act, w_first, w_second)
    x, dy = (a.reshape(total_tokens, -1) for a in (x, dy))
    act, gp = (a.reshape(total_tokens, -1) for a in (act, gp))
    grad_first = contract_first(x, gp) * factor
    grad_second = contract_first(act, dy) * factor
    return (grad_input, grad_first, grad_second)


def solution(mesh):
    in_specs = (P("row", "col"), P("row", "col"), P("col", "row"), P("col", "row"), P("row", "col"))
    out_specs = (P("row", "col"), P("col", "row"), P("row", "col"))
    return jax.shard_map(
        functools.partial(on_device, mesh.shape["row"], mesh.shape["col"]),
        mesh=mesh, in_specs=in_specs, out_specs=out_specs, check_vma=False,
    )
```

```python
import functools
import math

import jax
import jax.numpy as jnp
from jax import lax
from jax.experimental import pallas as pl
from jax.experimental.pallas import tpu as pltpu
from jax.sharding import PartitionSpec as P

gelu_coef = 0.044715
inner_c = math.sqrt(2.0 / math.pi)
SUB = 2
STRIP = 16
MESH = pl.DeviceIdType.MESH


def tanh_of(p):
    return jnp.tanh(inner_c * (p + gelu_coef * p * p * p))


def act_of(p):
    return 0.5 * p * (1.0 + tanh_of(p))


def slope_of(p):
    t = tanh_of(p)
    return 0.5 * (1.0 + t) + 0.5 * p * (1.0 - t * t) * inner_c * (1.0 + 3.0 * gelu_coef * p * p)


def contract_last(left, right):
    return lax.dot_general(
        left, right, (((1,), (1,)), ((), ())), preferred_element_type=jnp.float32
    )


def contract_first(left, right):
    return lax.dot_general(
        left, right, (((0,), (0,)), ((), ())), preferred_element_type=jnp.float32
    )


def strips(first, count, body):
    def one(i, carry):
        body(pl.ds(pl.multiple_of(first + i * STRIP, STRIP), STRIP))
        return carry

    lax.fori_loop(0, count // STRIP, one, 0)


def kernel(
    R, N,
    x_ref, dy_ref, pre_ref, w1_ref, w2_ref,
    gi_out, gs_out, gf_out, xf_out, gpf_out,
    w1, w2, dy, x, hid, pre, gp, act, slope, rs, gi_send, gi_recv, acc, gf,
    loc, out_sem, dy_s, dy_r, x_s, x_r, fw_s, pr_s, pr_r, rs_s, rs_r, gp_s, gp_r, gi_s, gi_r,
):
    r = lax.axis_index("row")
    c = lax.axis_index("col")
    q = R // N
    Tr = dy_ref.shape[0]
    Tc, H = pre_ref.shape
    Dc = dy_ref.shape[1]
    part = Tc // SUB
    last = N - 1
    f32, bf16 = jnp.float32, jnp.bfloat16

    barrier = pltpu.get_barrier_semaphore()
    for k in range(1, R):
        pl.semaphore_signal(barrier, inc=1, device_id={"row": lax.rem(r + k, R)}, device_id_type=MESH)

    @pl.when(c > 0)
    def _():
        pl.semaphore_signal(barrier, inc=1, device_id={"col": c - 1}, device_id_type=MESH)

    @pl.when(c < last)
    def _():
        pl.semaphore_signal(barrier, inc=1, device_id={"col": c + 1}, device_id_type=MESH)

    local = [
        pltpu.make_async_copy(dy_ref, dy.at[r], loc.at[0]),
        pltpu.make_async_copy(pre_ref, pre.at[c], loc.at[1]),
        pltpu.make_async_copy(w2_ref, w2, loc.at[2]),
        pltpu.make_async_copy(w1_ref, w1, loc.at[3]),
        pltpu.make_async_copy(x_ref, x.at[r], loc.at[4]),
    ]
    for copy in local:
        copy.start()
    ends = jnp.where(c > 0, 1, 0) + jnp.where(c < last, 1, 0)
    pl.semaphore_wait(barrier, R - 1 + ends)

    sibling = r + 1 - 2 * lax.rem(r, 2)
    chips = R // 2

    def row_send(src, dst, k, send, recv):
        to = sibling if k == 0 else lax.rem(r + 2 * k, R)
        return pltpu.make_async_remote_copy(
            src_ref=src, dst_ref=dst.at[r], send_sem=send.at[k], recv_sem=recv.at[r],
            device_id={"row": to}, device_id_type=MESH)

    def row_got(src, dst, p, send, recv):
        return pltpu.make_async_remote_copy(
            src_ref=src, dst_ref=dst.at[p], send_sem=send, recv_sem=recv.at[p],
            device_id={"row": sibling}, device_id_type=MESH)

    def row_forward(which, dst, k, recv):
        p = lax.rem(r + 2 * k, R)
        return pltpu.make_async_remote_copy(
            src_ref=dst.at[p], dst_ref=dst.at[p], send_sem=fw_s.at[which, k], recv_sem=recv.at[p],
            device_id={"row": sibling}, device_id_type=MESH)

    def row_start(src, dst, send, recv):
        for k in list(range(1, chips)) + [0]:
            row_send(src, dst, k, send, recv).start()

    def row_pass(which, src, dst, send, recv):
        for k in range(1, chips):
            row_got(src, dst, lax.rem(r + 2 * k, R), send.at[k], recv).wait_recv()
            row_forward(which, dst, k, recv).start()

    def row_rest(src, dst, send, recv):
        for k in range(chips):
            row_got(src, dst, lax.rem(sibling + 2 * k, R), send.at[k], recv).wait_recv()

    def row_end(which, src, dst, send, recv):
        for k in range(chips):
            row_send(src, dst, k, send, recv).wait_send()
            if k > 0:
                row_forward(which, dst, k, recv).wait_send()

    def sends_to(side):
        return c + 1 if side == 0 else c - 1

    def ag_shard(side, k):
        return c - k if side == 0 else c + k

    def ag_sends(side, k):
        return (c < last) & (c >= k) if side == 0 else (c > 0) & (c + k <= last)

    def ag_gets(side, k):
        return c >= k + 1 if side == 0 else c + 1 + k <= last

    def ag_got(side, k):
        return c - 1 - k if side == 0 else c + 1 + k

    def ag_copy(buf, shard, rows, side, send, recv, src=None):
        place = buf.at[shard] if rows is None else buf.at[shard, rows]
        return pltpu.make_async_remote_copy(
            src_ref=place if src is None else src, dst_ref=place, send_sem=send, recv_sem=recv,
            device_id={"col": sends_to(side)}, device_id_type=MESH)

    def rs_shard(side, k):
        return last - k + c if side == 0 else k - last + c

    def rs_sends(side, k):
        return c <= k if side == 0 else last - c <= k

    def rs_copy(side, k, j):
        rows = pl.ds(j * part, part)
        return pltpu.make_async_remote_copy(
            src_ref=hid.at[rs_shard(side, k), rows], dst_ref=rs.at[side, k, rows],
            send_sem=rs_s.at[side, k, j], recv_sem=rs_r.at[side, k, j],
            device_id={"col": sends_to(side)}, device_id_type=MESH)

    def rs_arrived(side, k, j):
        rows = pl.ds(j * part, part)
        return pltpu.make_async_remote_copy(
            src_ref=hid.at[c, rows], dst_ref=rs.at[side, k, rows],
            send_sem=rs_s.at[side, k, j], recv_sem=rs_r.at[side, k, j],
            device_id={"col": sends_to(side)}, device_id_type=MESH)

    def pre_step(k):
        for side in range(2):
            @pl.when(ag_sends(side, k))
            def _():
                if k > 0:
                    ag_copy(pre, ag_shard(side, k), None, side, pr_s.at[side, k - 1],
                            pr_r.at[side, k - 1]).wait_recv()
                ag_copy(pre, ag_shard(side, k), None, side, pr_s.at[side, k], pr_r.at[side, k],
                        pre_ref if k == 0 else None).start()

    row_start(dy_ref, dy, dy_s, dy_r)
    pre_step(0)

    local[1].wait()

    def slope_strip(rows):
        slope[rows, :] = slope_of(pre[c, rows, :].astype(f32))

    strips(0, Tc, slope_strip)

    local[0].wait()
    local[2].wait()
    row_pass(0, dy_ref, dy, dy_s, dy_r)
    row_rest(dy_ref, dy, dy_s, dy_r)
    row_start(x_ref, x, x_s, x_r)

    tile_h = min(512, H)

    def partial(s):
        def one(i, carry):
            cols = pl.ds(pl.multiple_of(i * tile_h, tile_h), tile_h)
            left = dy[q * s : q * s + q].reshape(Tc, Dc)
            hid[s, :, cols] = contract_last(left, w2[cols, :]).astype(bf16)
            return carry

        lax.fori_loop(0, H // tile_h, one, 0)

    order = []
    for i in range((N + 1) // 2):
        order += [last - i] + ([i] if i != last - i else [])
    for s in order:
        partial(s)
        if s == last:
            @pl.when(c == 0)
            def _():
                for j in range(SUB):
                    rs_copy(0, 0, j).start()
        if s == 0:
            @pl.when(c == last)
            def _():
                for j in range(SUB):
                    rs_copy(1, 0, j).start()

    def act_block(s):
        def one(rows):
            act[s, rows, :] = act_of(pre[s, rows, :].astype(f32)).astype(bf16)

        strips(0, Tc, one)

    def act_step(k):
        for side in range(2):
            @pl.when(ag_gets(side, k))
            def _():
                s = ag_got(side, k)
                forwarded = ag_sends(side, k + 1) if k + 1 < last else c < 0

                @pl.when(jnp.logical_not(forwarded))
                def _():
                    ag_copy(pre, s, None, side, pr_s.at[side, k], pr_r.at[side, k]).wait_recv()

                act_block(s)

    pre_step(1)
    act_block(c)
    for k in range(1, last):
        for j in range(SUB):
            for side in range(2):
                edge = c == 0 if side == 0 else c == last

                @pl.when(rs_sends(side, k) & jnp.logical_not(edge))
                def _():
                    rs_arrived(side, k - 1, j).wait_recv()
                    s = rs_shard(side, k)

                    def add(rows):
                        total = hid[s, rows, :].astype(f32) + rs[side, k - 1, rows, :].astype(f32)
                        hid[s, rows, :] = total.astype(bf16)

                    strips(j * part, part, add)

                @pl.when(rs_sends(side, k))
                def _():
                    @pl.when(rs_sends(side, k - 1))
                    def _():
                        rs_copy(side, k - 1, j).wait_send()

                    rs_copy(side, k, j).start()
        if k + 1 < last:
            pre_step(k + 1)
        if k == 1:
            row_pass(1, x_ref, x, x_s, x_r)
        act_step(k - 1)

    for j in range(SUB):
        rows_j = pl.ds(j * part, part)

        def load(rows):
            acc[rows, :] = hid[c, rows, :].astype(f32)

        strips(j * part, part, load)
        for side in range(2):
            @pl.when(c > 0 if side == 0 else c < last)
            def _():
                rs_arrived(side, last - 1, j).wait_recv()

                def add(rows):
                    acc[rows, :] = acc[rows, :] + rs[side, last - 1, rows, :].astype(f32)

                strips(j * part, part, add)

        def scale(rows):
            gp[c, rows, :] = (acc[rows, :] * slope[rows, :]).astype(bf16)

        strips(j * part, part, scale)
        for side in range(2):
            @pl.when(ag_sends(side, 0))
            def _():
                ag_copy(gp, c, rows_j, side, gp_s.at[side, 0, j], gp_r.at[side, 0, j]).start()

    local[3].wait()
    tile_d = min(512, Dc)

    def gi_copy(s, i):
        to = q * s + i
        return pltpu.make_async_remote_copy(
            src_ref=gi_send.at[s, pl.ds(i * Tr, Tr)], dst_ref=gi_recv.at[r],
            send_sem=gi_s.at[to], recv_sem=gi_r.at[r], device_id={"row": to}, device_id_type=MESH)

    def use_block(s):
        def one(i, carry):
            cols = pl.ds(pl.multiple_of(i * tile_d, tile_d), tile_d)
            gi_send[s, :, cols] = contract_last(gp[s], w1[cols, :]).astype(bf16)
            return carry

        lax.fori_loop(0, Dc // tile_d, one, 0)
        for i in range(q):
            to = q * s + i

            @pl.when(to != r)
            def _():
                gi_copy(s, i).start()

            @pl.when(to == r)
            def _():
                gi_recv[r] = gi_send[s, pl.ds(i * Tr, Tr), :]

    far = jnp.where(c < N // 2, last, 0)

    def gf_block(s, first):
        left = x[pl.ds(q * s, q)].reshape(Tc, Dc)

        def one(i, carry):
            cols = pl.ds(pl.multiple_of(i * tile_h, tile_h), tile_h)
            term = contract_first(left, gp[s, :, cols])
            gf[:, cols] = term if first else gf[:, cols] + term
            return carry

        lax.fori_loop(0, H // tile_h, one, 0)

    def gs_all():
        def one(i, carry):
            rows = pl.ds(pl.multiple_of(i * tile_g, tile_g), tile_g)
            left = act[:, :, rows].reshape(N * Tc, tile_g)
            w2[rows, :] = contract_first(left, dy[...].reshape(N * Tc, Dc)).astype(bf16)
            return carry

        lax.fori_loop(0, H // tile_g, one, 0)

    tile_g = min(256, H)
    gs_copy = pltpu.make_async_copy(w2, gs_out, out_sem.at[0])
    gf_copy = pltpu.make_async_copy(gf, gf_out, out_sem.at[1])
    xf_copy = pltpu.make_async_copy(x.at[pl.ds(q * far, q)], xf_out, out_sem.at[2])
    gpf_copy = pltpu.make_async_copy(gp.at[far], gpf_out, out_sem.at[3])
    use_block(c)
    act_step(last - 1)
    local[4].wait()
    row_rest(x_ref, x, x_s, x_r)
    xf_copy.start()
    gf_block(c, True)

    for k in range(last):
        for j in range(SUB):
            rows_j = pl.ds(j * part, part)
            for side in range(2):
                @pl.when(ag_gets(side, k))
                def _():
                    s = ag_got(side, k)
                    ag_copy(gp, s, rows_j, side, gp_s.at[side, k, j], gp_r.at[side, k, j]).wait_recv()
                    if k + 1 < last:
                        @pl.when(ag_sends(side, k + 1))
                        def _():
                            ag_copy(gp, s, rows_j, side, gp_s.at[side, k + 1, j],
                                    gp_r.at[side, k + 1, j]).start()
        for side in range(2):
            @pl.when(ag_gets(side, k))
            def _():
                s = ag_got(side, k)
                use_block(s)

                @pl.when(s == far)
                def _():
                    gpf_copy.start()

                if k + 1 < last:
                    @pl.when(s != far)
                    def _():
                        gf_block(s, False)
        if k == 0:
            gs_all()
            gs_copy.start()
        if k == last - 2:
            gf_copy.start()

    for k in range(1, R):
        p = lax.rem(r + k, R)
        row_got(gi_send.at[0, pl.ds(0, Tr)], gi_recv, p, gi_s.at[p], gi_r).wait_recv()

    def total_strip(rows):
        total = gi_recv[0, rows, :].astype(f32)
        for p in range(1, R):
            total = total + gi_recv[p, rows, :].astype(f32)
        gi_out[rows, :] = total.astype(bf16)

    strips(0, Tr, total_strip)

    row_end(0, dy_ref, dy, dy_s, dy_r)
    row_end(1, x_ref, x, x_s, x_r)
    for s in range(N):
        for i in range(q):
            @pl.when(q * s + i != r)
            def _():
                gi_copy(s, i).wait_send()
    for side in range(2):
        for k in range(last):
            @pl.when(ag_sends(side, k))
            def _():
                s = ag_shard(side, k)
                ag_copy(pre, s, None, side, pr_s.at[side, k], pr_r.at[side, k],
                        pre_ref if k == 0 else None).wait_send()
                for j in range(SUB):
                    ag_copy(gp, s, pl.ds(j * part, part), side, gp_s.at[side, k, j],
                            gp_r.at[side, k, j]).wait_send()

        @pl.when(rs_sends(side, last - 1))
        def _():
            for j in range(SUB):
                rs_copy(side, last - 1, j).wait_send()
    for copy in (gs_copy, gf_copy, xf_copy, gpf_copy):
        copy.wait()


def exchange(R, N, x, dy, pre, w1, w2):
    Tr, Dc = dy.shape
    Tc, H = pre.shape
    bf16 = jnp.bfloat16
    dma = pltpu.SemaphoreType.DMA
    hbm = pl.BlockSpec(memory_space=pl.ANY)
    return pl.pallas_call(
        functools.partial(kernel, R, N),
        out_shape=[
            jax.ShapeDtypeStruct((Tr, Dc), bf16),
            jax.ShapeDtypeStruct((H, Dc), bf16),
            jax.ShapeDtypeStruct((Dc, H), jnp.float32),
            jax.ShapeDtypeStruct((R // N, Tr, Dc), bf16),
            jax.ShapeDtypeStruct((Tc, H), bf16),
        ],
        in_specs=[hbm] * 5,
        out_specs=[pl.BlockSpec(memory_space=pltpu.VMEM)] + [hbm] * 4,
        scratch_shapes=[
            pltpu.VMEM(w1.shape, bf16),
            pltpu.VMEM(w2.shape, bf16),
            pltpu.VMEM((R, Tr, Dc), bf16),
            pltpu.VMEM((R, Tr, Dc), bf16),
            pltpu.VMEM((N, Tc, H), bf16),
            pltpu.VMEM((N, Tc, H), bf16),
            pltpu.VMEM((N, Tc, H), bf16),
            pltpu.VMEM((N, Tc, H), bf16),
            pltpu.VMEM((Tc, H), jnp.float32),
            pltpu.VMEM((2, N - 1, Tc, H), bf16),
            pltpu.VMEM((N, Tc, Dc), bf16),
            pltpu.VMEM((R, Tr, Dc), bf16),
            pltpu.VMEM((Tc, H), jnp.float32),
            pltpu.VMEM((Dc, H), jnp.float32),
            dma((5,)),
            dma((4,)),
            dma((R // 2,)), dma((R,)), dma((R // 2,)), dma((R,)), dma((2, R // 2)),
            dma((2, N - 1)), dma((2, N - 1)),
            dma((2, N - 1, SUB)), dma((2, N - 1, SUB)),
            dma((2, N - 1, SUB)), dma((2, N - 1, SUB)),
            dma((R,)), dma((R,)),
        ],
        compiler_params=pltpu.CompilerParams(
            collective_id=0, has_side_effects=True, vmem_limit_bytes=60 * 2**20
        ),
    )(x, dy, pre, w1, w2)


def on_device(R, N, inputs_act, out_grad, pre_act, w_first, w_second):
    total_tokens = pre_act.shape[0] * N
    factor = 1.0 / math.sqrt(total_tokens)
    grad_input, gs, gf, x_far, gp_far = exchange(
        R, N, inputs_act, out_grad, pre_act, w_first, w_second
    )
    x_far = x_far.reshape(gp_far.shape[0], -1)
    grad_first = (gf + contract_first(x_far, gp_far)) * factor
    grad_second = gs.astype(jnp.float32) * factor
    return (grad_input, grad_first, grad_second)


def solution(mesh):
    in_specs = (P("row", "col"), P("row", "col"), P("col", "row"), P("col", "row"), P("row", "col"))
    out_specs = (P("row", "col"), P("col", "row"), P("row", "col"))
    return jax.shard_map(
        functools.partial(on_device, mesh.shape["row"], mesh.shape["col"]),
        mesh=mesh, in_specs=in_specs, out_specs=out_specs, check_vma=False,
    )
```

```python
import functools
import math

import jax
import jax.numpy as jnp
from jax import lax
from jax.experimental import pallas as pl
from jax.experimental.pallas import tpu as pltpu
from jax.sharding import PartitionSpec as P

gelu_coef = 0.044715
inner_c = math.sqrt(2.0 / math.pi)
STRIP = 16
MESH = pl.DeviceIdType.MESH


def tanh_of(p):
    return jnp.tanh(inner_c * (p + gelu_coef * p * p * p))


def act_of(p):
    return 0.5 * p * (1.0 + tanh_of(p))


def slope_of(p):
    t = tanh_of(p)
    return 0.5 * (1.0 + t) + 0.5 * p * (1.0 - t * t) * inner_c * (1.0 + 3.0 * gelu_coef * p * p)


def contract_last(left, right):
    return lax.dot_general(
        left, right, (((1,), (1,)), ((), ())), preferred_element_type=jnp.float32
    )


def contract_first(left, right):
    return lax.dot_general(
        left, right, (((0,), (0,)), ((), ())), preferred_element_type=jnp.float32
    )


def strips(first, count, body):
    def one(i, carry):
        body(pl.ds(pl.multiple_of(first + i * STRIP, STRIP), STRIP))
        return carry

    lax.fori_loop(0, count // STRIP, one, 0)


def kernel(
    R, N,
    x_ref, dy_ref, pre_ref, w1_ref, w2_ref,
    gi_out, gs_out, gf_out,
    w1, w2, dy, x, hid, pre, gp, act, slope, rs, gi_send, gi_recv, acc, gf, gf_half,
    loc, out_sem, dy_s, dy_r, x_s, x_r, fw_s, pr_s, pr_r, rs_s, rs_r, gp_s, gp_r, gi_s, gi_r,
):
    r = lax.axis_index("row")
    c = lax.axis_index("col")
    q = SUB = R // N
    Tr = dy_ref.shape[0]
    Tc, H = pre_ref.shape
    Dc = dy_ref.shape[1]
    part = Tc // SUB
    last = N - 1
    f32, bf16 = jnp.float32, jnp.bfloat16

    barrier = pltpu.get_barrier_semaphore()
    for k in range(1, R):
        pl.semaphore_signal(barrier, inc=1, device_id={"row": lax.rem(r + k, R)}, device_id_type=MESH)

    @pl.when(c > 0)
    def _():
        pl.semaphore_signal(barrier, inc=1, device_id={"col": c - 1}, device_id_type=MESH)

    @pl.when(c < last)
    def _():
        pl.semaphore_signal(barrier, inc=1, device_id={"col": c + 1}, device_id_type=MESH)

    local = [
        pltpu.make_async_copy(dy_ref, dy.at[r], loc.at[0]),
        pltpu.make_async_copy(pre_ref, pre.at[c], loc.at[1]),
        pltpu.make_async_copy(w2_ref, w2, loc.at[2]),
        pltpu.make_async_copy(w1_ref, w1, loc.at[3]),
        pltpu.make_async_copy(x_ref, x.at[r], loc.at[4]),
    ]
    for copy in local:
        copy.start()
    ends = jnp.where(c > 0, 1, 0) + jnp.where(c < last, 1, 0)
    pl.semaphore_wait(barrier, R - 1 + ends)

    sibling = r + 1 - 2 * lax.rem(r, 2)
    chips = R // 2

    def row_send(src, dst, k, send, recv):
        to = sibling if k == 0 else lax.rem(r + 2 * k, R)
        return pltpu.make_async_remote_copy(
            src_ref=src, dst_ref=dst.at[r], send_sem=send.at[k], recv_sem=recv.at[r],
            device_id={"row": to}, device_id_type=MESH)

    def row_got(src, dst, p, send, recv):
        return pltpu.make_async_remote_copy(
            src_ref=src, dst_ref=dst.at[p], send_sem=send, recv_sem=recv.at[p],
            device_id={"row": sibling}, device_id_type=MESH)

    def row_forward(which, dst, k, recv):
        p = lax.rem(r + 2 * k, R)
        return pltpu.make_async_remote_copy(
            src_ref=dst.at[p], dst_ref=dst.at[p], send_sem=fw_s.at[which, k], recv_sem=recv.at[p],
            device_id={"row": sibling}, device_id_type=MESH)

    def row_start(src, dst, send, recv):
        for k in list(range(1, chips)) + [0]:
            row_send(src, dst, k, send, recv).start()

    def row_pass(which, src, dst, send, recv):
        for k in range(1, chips):
            row_got(src, dst, lax.rem(r + 2 * k, R), send.at[k], recv).wait_recv()
            row_forward(which, dst, k, recv).start()

    def row_rest(src, dst, send, recv):
        for k in range(chips):
            row_got(src, dst, lax.rem(sibling + 2 * k, R), send.at[k], recv).wait_recv()

    def row_end(which, src, dst, send, recv):
        for k in range(chips):
            row_send(src, dst, k, send, recv).wait_send()
            if k > 0:
                row_forward(which, dst, k, recv).wait_send()

    def sends_to(side):
        return c + 1 if side == 0 else c - 1

    def ag_shard(side, k):
        return c - k if side == 0 else c + k

    def ag_sends(side, k):
        return (c < last) & (c >= k) if side == 0 else (c > 0) & (c + k <= last)

    def ag_gets(side, k):
        return c >= k + 1 if side == 0 else c + 1 + k <= last

    def ag_got(side, k):
        return c - 1 - k if side == 0 else c + 1 + k

    def ag_copy(buf, shard, rows, side, send, recv, src=None):
        place = buf.at[shard] if rows is None else buf.at[shard, rows]
        return pltpu.make_async_remote_copy(
            src_ref=place if src is None else src, dst_ref=place, send_sem=send, recv_sem=recv,
            device_id={"col": sends_to(side)}, device_id_type=MESH)

    def rs_shard(side, k):
        return last - k + c if side == 0 else k - last + c

    def rs_sends(side, k):
        return c <= k if side == 0 else last - c <= k

    def rs_copy(side, k, j):
        rows = pl.ds(j * part, part)
        return pltpu.make_async_remote_copy(
            src_ref=hid.at[rs_shard(side, k), rows], dst_ref=rs.at[side, k, rows],
            send_sem=rs_s.at[side, k, j], recv_sem=rs_r.at[side, k, j],
            device_id={"col": sends_to(side)}, device_id_type=MESH)

    def rs_arrived(side, k, j):
        rows = pl.ds(j * part, part)
        return pltpu.make_async_remote_copy(
            src_ref=hid.at[c, rows], dst_ref=rs.at[side, k, rows],
            send_sem=rs_s.at[side, k, j], recv_sem=rs_r.at[side, k, j],
            device_id={"col": sends_to(side)}, device_id_type=MESH)

    def pre_step(k):
        for side in range(2):
            @pl.when(ag_sends(side, k))
            def _():
                if k > 0:
                    ag_copy(pre, ag_shard(side, k), None, side, pr_s.at[side, k - 1],
                            pr_r.at[side, k - 1]).wait_recv()
                ag_copy(pre, ag_shard(side, k), None, side, pr_s.at[side, k], pr_r.at[side, k],
                        pre_ref if k == 0 else None).start()

    row_start(dy_ref, dy, dy_s, dy_r)
    pre_step(0)

    local[1].wait()

    def slope_strip(rows):
        slope[rows, :] = slope_of(pre[c, rows, :].astype(f32))

    strips(0, Tc, slope_strip)

    local[0].wait()
    local[2].wait()
    row_pass(0, dy_ref, dy, dy_s, dy_r)
    row_rest(dy_ref, dy, dy_s, dy_r)
    row_start(x_ref, x, x_s, x_r)

    tile_h = min(512, H)

    def partial(s):
        def one(i, carry):
            cols = pl.ds(pl.multiple_of(i * tile_h, tile_h), tile_h)
            left = dy[q * s : q * s + q].reshape(Tc, Dc)
            hid[s, :, cols] = contract_last(left, w2[cols, :]).astype(bf16)
            return carry

        lax.fori_loop(0, H // tile_h, one, 0)

    order = []
    for i in range((N + 1) // 2):
        order += [last - i] + ([i] if i != last - i else [])
    for s in order:
        partial(s)
        if s == last:
            @pl.when(c == 0)
            def _():
                for j in range(SUB):
                    rs_copy(0, 0, j).start()
        if s == 0:
            @pl.when(c == last)
            def _():
                for j in range(SUB):
                    rs_copy(1, 0, j).start()

    def act_block(s):
        def one(rows):
            act[s, rows, :] = act_of(pre[s, rows, :].astype(f32)).astype(bf16)

        strips(0, Tc, one)

    def act_step(k):
        for side in range(2):
            @pl.when(ag_gets(side, k))
            def _():
                s = ag_got(side, k)
                forwarded = ag_sends(side, k + 1) if k + 1 < last else c < 0

                @pl.when(jnp.logical_not(forwarded))
                def _():
                    ag_copy(pre, s, None, side, pr_s.at[side, k], pr_r.at[side, k]).wait_recv()

                act_block(s)

    pre_step(1)
    act_block(c)
    for k in range(1, last):
        for j in range(SUB):
            for side in range(2):
                edge = c == 0 if side == 0 else c == last

                @pl.when(rs_sends(side, k) & jnp.logical_not(edge))
                def _():
                    rs_arrived(side, k - 1, j).wait_recv()
                    s = rs_shard(side, k)

                    def add(rows):
                        total = hid[s, rows, :].astype(f32) + rs[side, k - 1, rows, :].astype(f32)
                        hid[s, rows, :] = total.astype(bf16)

                    strips(j * part, part, add)

                @pl.when(rs_sends(side, k))
                def _():
                    @pl.when(rs_sends(side, k - 1))
                    def _():
                        rs_copy(side, k - 1, j).wait_send()

                    rs_copy(side, k, j).start()
        if k + 1 < last:
            pre_step(k + 1)
        if k == 1:
            row_pass(1, x_ref, x, x_s, x_r)
        act_step(k - 1)

    for j in range(SUB):
        rows_j = pl.ds(j * part, part)

        def load(rows):
            acc[rows, :] = hid[c, rows, :].astype(f32)

        strips(j * part, part, load)
        for side in range(2):
            @pl.when(c > 0 if side == 0 else c < last)
            def _():
                rs_arrived(side, last - 1, j).wait_recv()

                def add(rows):
                    acc[rows, :] = acc[rows, :] + rs[side, last - 1, rows, :].astype(f32)

                strips(j * part, part, add)

        def scale(rows):
            gp[c, rows, :] = (acc[rows, :] * slope[rows, :]).astype(bf16)

        strips(j * part, part, scale)
        for side in range(2):
            @pl.when(ag_sends(side, 0))
            def _():
                ag_copy(gp, c, rows_j, side, gp_s.at[side, 0, j], gp_r.at[side, 0, j]).start()

    local[3].wait()
    tile_d = min(512, Dc)

    def gi_copy(s, i):
        to = q * s + i
        return pltpu.make_async_remote_copy(
            src_ref=gi_send.at[s, pl.ds(i * Tr, Tr)], dst_ref=gi_recv.at[r],
            send_sem=gi_s.at[to], recv_sem=gi_r.at[r], device_id={"row": to}, device_id_type=MESH)

    def use_piece(s, i):
        rows = pl.ds(i * Tr, Tr)

        def one(t, carry):
            cols = pl.ds(pl.multiple_of(t * tile_d, tile_d), tile_d)
            gi_send[s, rows, cols] = contract_last(gp[s, rows, :], w1[cols, :]).astype(bf16)
            return carry

        lax.fori_loop(0, Dc // tile_d, one, 0)
        to = q * s + i

        @pl.when(to != r)
        def _():
            gi_copy(s, i).start()

        @pl.when(to == r)
        def _():
            gi_recv[r] = gi_send[s, rows, :]

    far = jnp.where(c < N // 2, last, 0)

    def gf_block(s, first, end=False):
        left = x[pl.ds(q * s, q)].reshape(Tc, Dc)

        def one(i, carry):
            cols = pl.ds(pl.multiple_of(i * tile_h, tile_h), tile_h)
            term = contract_first(left, gp[s, :, cols])
            if end:
                gf_half[:, cols] = (gf[:, cols] + term).astype(bf16)
            else:
                gf[:, cols] = term if first else gf[:, cols] + term
            return carry

        lax.fori_loop(0, H // tile_h, one, 0)

    def gs_all():
        def one(i, carry):
            rows = pl.ds(pl.multiple_of(i * tile_g, tile_g), tile_g)
            left = act[:, :, rows].reshape(N * Tc, tile_g)
            w2[rows, :] = contract_first(left, dy[...].reshape(N * Tc, Dc)).astype(bf16)
            return carry

        lax.fori_loop(0, H // tile_g, one, 0)

    tile_g = min(256, H)
    gs_copy = pltpu.make_async_copy(w2, gs_out, out_sem.at[0])
    gf_copy = pltpu.make_async_copy(gf_half, gf_out, out_sem.at[1])
    for i in range(q):
        use_piece(c, i)
    act_step(last - 1)
    local[4].wait()
    row_rest(x_ref, x, x_s, x_r)
    gf_block(c, True)

    for k in range(last):
        for j in range(SUB):
            rows_j = pl.ds(j * part, part)
            for side in range(2):
                @pl.when(ag_gets(side, k))
                def _():
                    s = ag_got(side, k)
                    ag_copy(gp, s, rows_j, side, gp_s.at[side, k, j], gp_r.at[side, k, j]).wait_recv()
                    if k + 1 < last:
                        @pl.when(ag_sends(side, k + 1))
                        def _():
                            ag_copy(gp, s, rows_j, side, gp_s.at[side, k + 1, j],
                                    gp_r.at[side, k + 1, j]).start()
            for side in range(2):
                @pl.when(ag_gets(side, k))
                def _():
                    use_piece(ag_got(side, k), j)
        if k + 1 < last:
            for side in range(2):
                s = ag_got(side, k)

                @pl.when(ag_gets(side, k) & (s != far))
                def _():
                    gf_block(s, False)
        if k == 0:
            gs_all()
            gs_copy.start()
    gf_block(far, False, True)
    gf_copy.start()

    for k in range(1, R):
        p = lax.rem(r + k, R)
        row_got(gi_send.at[0, pl.ds(0, Tr)], gi_recv, p, gi_s.at[p], gi_r).wait_recv()

    def total_strip(rows):
        total = gi_recv[0, rows, :].astype(f32)
        for p in range(1, R):
            total = total + gi_recv[p, rows, :].astype(f32)
        gi_out[rows, :] = total.astype(bf16)

    strips(0, Tr, total_strip)

    row_end(0, dy_ref, dy, dy_s, dy_r)
    row_end(1, x_ref, x, x_s, x_r)
    for s in range(N):
        for i in range(q):
            @pl.when(q * s + i != r)
            def _():
                gi_copy(s, i).wait_send()
    for side in range(2):
        for k in range(last):
            @pl.when(ag_sends(side, k))
            def _():
                s = ag_shard(side, k)
                ag_copy(pre, s, None, side, pr_s.at[side, k], pr_r.at[side, k],
                        pre_ref if k == 0 else None).wait_send()
                for j in range(SUB):
                    ag_copy(gp, s, pl.ds(j * part, part), side, gp_s.at[side, k, j],
                            gp_r.at[side, k, j]).wait_send()

        @pl.when(rs_sends(side, last - 1))
        def _():
            for j in range(SUB):
                rs_copy(side, last - 1, j).wait_send()
    for copy in (gs_copy, gf_copy):
        copy.wait()


def exchange(R, N, x, dy, pre, w1, w2):
    Tr, Dc = dy.shape
    Tc, H = pre.shape
    SUB = R // N
    bf16 = jnp.bfloat16
    dma = pltpu.SemaphoreType.DMA
    hbm = pl.BlockSpec(memory_space=pl.ANY)
    return pl.pallas_call(
        functools.partial(kernel, R, N),
        out_shape=[
            jax.ShapeDtypeStruct((Tr, Dc), bf16),
            jax.ShapeDtypeStruct((H, Dc), bf16),
            jax.ShapeDtypeStruct((Dc, H), bf16),
        ],
        in_specs=[hbm] * 5,
        out_specs=[pl.BlockSpec(memory_space=pltpu.VMEM)] + [hbm] * 2,
        scratch_shapes=[
            pltpu.VMEM(w1.shape, bf16),
            pltpu.VMEM(w2.shape, bf16),
            pltpu.VMEM((R, Tr, Dc), bf16),
            pltpu.VMEM((R, Tr, Dc), bf16),
            pltpu.VMEM((N, Tc, H), bf16),
            pltpu.VMEM((N, Tc, H), bf16),
            pltpu.VMEM((N, Tc, H), bf16),
            pltpu.VMEM((N, Tc, H), bf16),
            pltpu.VMEM((Tc, H), jnp.float32),
            pltpu.VMEM((2, N - 1, Tc, H), bf16),
            pltpu.VMEM((N, Tc, Dc), bf16),
            pltpu.VMEM((R, Tr, Dc), bf16),
            pltpu.VMEM((Tc, H), jnp.float32),
            pltpu.VMEM((Dc, H), jnp.float32),
            pltpu.VMEM((Dc, H), bf16),
            dma((5,)),
            dma((2,)),
            dma((R // 2,)), dma((R,)), dma((R // 2,)), dma((R,)), dma((2, R // 2)),
            dma((2, N - 1)), dma((2, N - 1)),
            dma((2, N - 1, SUB)), dma((2, N - 1, SUB)),
            dma((2, N - 1, SUB)), dma((2, N - 1, SUB)),
            dma((R,)), dma((R,)),
        ],
        compiler_params=pltpu.CompilerParams(
            collective_id=0, has_side_effects=True, vmem_limit_bytes=60 * 2**20
        ),
    )(x, dy, pre, w1, w2)


def on_device(R, N, inputs_act, out_grad, pre_act, w_first, w_second):
    total_tokens = pre_act.shape[0] * N
    factor = 1.0 / math.sqrt(total_tokens)
    grad_input, gs, gf = exchange(R, N, inputs_act, out_grad, pre_act, w_first, w_second)
    grad_first = gf.astype(jnp.float32) * factor
    grad_second = gs.astype(jnp.float32) * factor
    return (grad_input, grad_first, grad_second)


def solution(mesh):
    in_specs = (P("row", "col"), P("row", "col"), P("col", "row"), P("col", "row"), P("row", "col"))
    out_specs = (P("row", "col"), P("col", "row"), P("row", "col"))
    return jax.shard_map(
        functools.partial(on_device, mesh.shape["row"], mesh.shape["col"]),
        mesh=mesh, in_specs=in_specs, out_specs=out_specs, check_vma=False,
    )
```

```python
import functools
import math

import jax
import jax.numpy as jnp
from jax import lax
from jax.experimental import pallas as pl
from jax.experimental.pallas import tpu as pltpu
from jax.sharding import PartitionSpec as P

gelu_coef = 0.044715
inner_c = math.sqrt(2.0 / math.pi)
STRIP = 16
MESH = pl.DeviceIdType.MESH


def tanh_of(p):
    return jnp.tanh(inner_c * (p + gelu_coef * p * p * p))


def act_of(p):
    return 0.5 * p * (1.0 + tanh_of(p))


def slope_of(p):
    t = tanh_of(p)
    return 0.5 * (1.0 + t) + 0.5 * p * (1.0 - t * t) * inner_c * (1.0 + 3.0 * gelu_coef * p * p)


def contract_last(left, right):
    return lax.dot_general(
        left, right, (((1,), (1,)), ((), ())), preferred_element_type=jnp.float32
    )


def contract_first(left, right):
    return lax.dot_general(
        left, right, (((0,), (0,)), ((), ())), preferred_element_type=jnp.float32
    )


def strips(first, count, body):
    def one(i, carry):
        body(pl.ds(pl.multiple_of(first + i * STRIP, STRIP), STRIP))
        return carry

    lax.fori_loop(0, count // STRIP, one, 0)


def kernel(
    R, N,
    x_ref, dy_ref, pre_ref, w1_ref, w2_ref,
    gi_out, gs_out, gf_out,
    w1, w2, dy, x, hid, pre, gp, act, slope, rs, gi_send, gi_recv, acc, gf, gf_half,
    loc, out_sem, dy_s, dy_r, x_s, x_r, fw_s, pr_s, pr_r, rs_s, rs_r, gp_s, gp_r, gi_s, gi_r,
):
    r = lax.axis_index("row")
    c = lax.axis_index("col")
    q = SUB = R // N
    Tr = dy_ref.shape[0]
    Tc, H = pre_ref.shape
    Dc = dy_ref.shape[1]
    part = Tc // SUB
    FINE = 2 * SUB
    fine = Tc // FINE
    last = N - 1
    f32, bf16 = jnp.float32, jnp.bfloat16

    barrier = pltpu.get_barrier_semaphore()
    for k in range(1, R):
        pl.semaphore_signal(barrier, inc=1, device_id={"row": lax.rem(r + k, R)}, device_id_type=MESH)

    @pl.when(c > 0)
    def _():
        pl.semaphore_signal(barrier, inc=1, device_id={"col": c - 1}, device_id_type=MESH)

    @pl.when(c < last)
    def _():
        pl.semaphore_signal(barrier, inc=1, device_id={"col": c + 1}, device_id_type=MESH)

    local = [
        pltpu.make_async_copy(dy_ref, dy.at[r], loc.at[0]),
        pltpu.make_async_copy(pre_ref, pre.at[c], loc.at[1]),
        pltpu.make_async_copy(w2_ref, w2, loc.at[2]),
        pltpu.make_async_copy(w1_ref, w1, loc.at[3]),
        pltpu.make_async_copy(x_ref, x.at[r], loc.at[4]),
    ]
    for copy in local:
        copy.start()
    ends = jnp.where(c > 0, 1, 0) + jnp.where(c < last, 1, 0)
    pl.semaphore_wait(barrier, R - 1 + ends)

    sibling = r + 1 - 2 * lax.rem(r, 2)
    chips = R // 2

    def row_send(src, dst, k, send, recv):
        to = sibling if k == 0 else lax.rem(r + 2 * k, R)
        return pltpu.make_async_remote_copy(
            src_ref=src, dst_ref=dst.at[r], send_sem=send.at[k], recv_sem=recv.at[r],
            device_id={"row": to}, device_id_type=MESH)

    def row_got(src, dst, p, send, recv):
        return pltpu.make_async_remote_copy(
            src_ref=src, dst_ref=dst.at[p], send_sem=send, recv_sem=recv.at[p],
            device_id={"row": sibling}, device_id_type=MESH)

    def row_forward(which, dst, k, recv):
        p = lax.rem(r + 2 * k, R)
        return pltpu.make_async_remote_copy(
            src_ref=dst.at[p], dst_ref=dst.at[p], send_sem=fw_s.at[which, k], recv_sem=recv.at[p],
            device_id={"row": sibling}, device_id_type=MESH)

    def row_start(src, dst, send, recv):
        for k in list(range(1, chips)) + [0]:
            row_send(src, dst, k, send, recv).start()

    def row_pass(which, src, dst, send, recv):
        for k in range(1, chips):
            row_got(src, dst, lax.rem(r + 2 * k, R), send.at[k], recv).wait_recv()
            row_forward(which, dst, k, recv).start()

    def row_rest(src, dst, send, recv):
        for k in range(chips):
            row_got(src, dst, lax.rem(sibling + 2 * k, R), send.at[k], recv).wait_recv()

    def row_end(which, src, dst, send, recv):
        for k in range(chips):
            row_send(src, dst, k, send, recv).wait_send()
            if k > 0:
                row_forward(which, dst, k, recv).wait_send()

    def sends_to(side):
        return c + 1 if side == 0 else c - 1

    def ag_shard(side, k):
        return c - k if side == 0 else c + k

    def ag_sends(side, k):
        return (c < last) & (c >= k) if side == 0 else (c > 0) & (c + k <= last)

    def ag_gets(side, k):
        return c >= k + 1 if side == 0 else c + 1 + k <= last

    def ag_got(side, k):
        return c - 1 - k if side == 0 else c + 1 + k

    def ag_copy(buf, shard, rows, side, send, recv, src=None):
        place = buf.at[shard] if rows is None else buf.at[shard, rows]
        return pltpu.make_async_remote_copy(
            src_ref=place if src is None else src, dst_ref=place, send_sem=send, recv_sem=recv,
            device_id={"col": sends_to(side)}, device_id_type=MESH)

    def rs_shard(side, k):
        return last - k + c if side == 0 else k - last + c

    def rs_sends(side, k):
        return c <= k if side == 0 else last - c <= k

    def rs_copy(side, k, j):
        rows = pl.ds(j * fine, fine)
        return pltpu.make_async_remote_copy(
            src_ref=hid.at[rs_shard(side, k), rows], dst_ref=rs.at[side, k, rows],
            send_sem=rs_s.at[side, k, j], recv_sem=rs_r.at[side, k, j],
            device_id={"col": sends_to(side)}, device_id_type=MESH)

    def rs_arrived(side, k, j):
        rows = pl.ds(j * fine, fine)
        return pltpu.make_async_remote_copy(
            src_ref=hid.at[c, rows], dst_ref=rs.at[side, k, rows],
            send_sem=rs_s.at[side, k, j], recv_sem=rs_r.at[side, k, j],
            device_id={"col": sends_to(side)}, device_id_type=MESH)

    def pre_step(k):
        for side in range(2):
            @pl.when(ag_sends(side, k))
            def _():
                if k > 0:
                    ag_copy(pre, ag_shard(side, k), None, side, pr_s.at[side, k - 1],
                            pr_r.at[side, k - 1]).wait_recv()
                ag_copy(pre, ag_shard(side, k), None, side, pr_s.at[side, k], pr_r.at[side, k],
                        pre_ref if k == 0 else None).start()

    row_start(dy_ref, dy, dy_s, dy_r)
    pre_step(0)

    local[1].wait()

    def slope_strip(rows):
        slope[rows, :] = slope_of(pre[c, rows, :].astype(f32))

    strips(0, Tc, slope_strip)

    local[0].wait()
    local[2].wait()
    row_pass(0, dy_ref, dy, dy_s, dy_r)
    row_rest(dy_ref, dy, dy_s, dy_r)
    row_start(x_ref, x, x_s, x_r)

    tile_h = min(512, H)

    def partial(s):
        def one(i, carry):
            cols = pl.ds(pl.multiple_of(i * tile_h, tile_h), tile_h)
            left = dy[q * s : q * s + q].reshape(Tc, Dc)
            hid[s, :, cols] = contract_last(left, w2[cols, :]).astype(bf16)
            return carry

        lax.fori_loop(0, H // tile_h, one, 0)

    order = []
    for i in range((N + 1) // 2):
        order += [last - i] + ([i] if i != last - i else [])
    for s in order:
        partial(s)
        if s == last:
            @pl.when(c == 0)
            def _():
                for j in range(FINE):
                    rs_copy(0, 0, j).start()
        if s == 0:
            @pl.when(c == last)
            def _():
                for j in range(FINE):
                    rs_copy(1, 0, j).start()

    def act_block(s):
        def one(rows):
            act[s, rows, :] = act_of(pre[s, rows, :].astype(f32)).astype(bf16)

        strips(0, Tc, one)

    def act_step(k):
        for side in range(2):
            @pl.when(ag_gets(side, k))
            def _():
                s = ag_got(side, k)
                forwarded = ag_sends(side, k + 1) if k + 1 < last else c < 0

                @pl.when(jnp.logical_not(forwarded))
                def _():
                    ag_copy(pre, s, None, side, pr_s.at[side, k], pr_r.at[side, k]).wait_recv()

                act_block(s)

    pre_step(1)
    act_block(c)
    for k in range(1, last):
        for j in range(FINE):
            for side in range(2):
                edge = c == 0 if side == 0 else c == last

                @pl.when(rs_sends(side, k) & jnp.logical_not(edge))
                def _():
                    rs_arrived(side, k - 1, j).wait_recv()
                    s = rs_shard(side, k)

                    def add(rows):
                        total = hid[s, rows, :].astype(f32) + rs[side, k - 1, rows, :].astype(f32)
                        hid[s, rows, :] = total.astype(bf16)

                    strips(j * fine, fine, add)

                @pl.when(rs_sends(side, k))
                def _():
                    @pl.when(rs_sends(side, k - 1))
                    def _():
                        rs_copy(side, k - 1, j).wait_send()

                    rs_copy(side, k, j).start()
        if k + 1 < last:
            pre_step(k + 1)
        if k == 1:
            row_pass(1, x_ref, x, x_s, x_r)
        act_step(k - 1)

    for j in range(SUB):
        rows_j = pl.ds(j * part, part)

        def load(rows):
            acc[rows, :] = hid[c, rows, :].astype(f32)

        strips(j * part, part, load)
        for side in range(2):
            @pl.when(c > 0 if side == 0 else c < last)
            def _():
                for piece in range(2 * j, 2 * j + 2):
                    rs_arrived(side, last - 1, piece).wait_recv()

                def add(rows):
                    acc[rows, :] = acc[rows, :] + rs[side, last - 1, rows, :].astype(f32)

                strips(j * part, part, add)

        def scale(rows):
            gp[c, rows, :] = (acc[rows, :] * slope[rows, :]).astype(bf16)

        strips(j * part, part, scale)
        for side in range(2):
            @pl.when(ag_sends(side, 0))
            def _():
                ag_copy(gp, c, rows_j, side, gp_s.at[side, 0, j], gp_r.at[side, 0, j]).start()

    local[3].wait()
    tile_d = min(512, Dc)

    def gi_copy(s, i):
        to = q * s + i
        return pltpu.make_async_remote_copy(
            src_ref=gi_send.at[s, pl.ds(i * Tr, Tr)], dst_ref=gi_recv.at[r],
            send_sem=gi_s.at[to], recv_sem=gi_r.at[r], device_id={"row": to}, device_id_type=MESH)

    def use_piece(s, i):
        rows = pl.ds(i * Tr, Tr)

        def one(t, carry):
            cols = pl.ds(pl.multiple_of(t * tile_d, tile_d), tile_d)
            gi_send[s, rows, cols] = contract_last(gp[s, rows, :], w1[cols, :]).astype(bf16)
            return carry

        lax.fori_loop(0, Dc // tile_d, one, 0)
        to = q * s + i

        @pl.when(to != r)
        def _():
            gi_copy(s, i).start()

        @pl.when(to == r)
        def _():
            gi_recv[r] = gi_send[s, rows, :]

    far = jnp.where(c < N // 2, last, 0)

    def gf_block(s, first, end=False):
        left = x[pl.ds(q * s, q)].reshape(Tc, Dc)

        def one(i, carry):
            cols = pl.ds(pl.multiple_of(i * tile_h, tile_h), tile_h)
            term = contract_first(left, gp[s, :, cols])
            if end:
                gf_half[:, cols] = (gf[:, cols] + term).astype(bf16)
            else:
                gf[:, cols] = term if first else gf[:, cols] + term
            return carry

        lax.fori_loop(0, H // tile_h, one, 0)

    def gs_all():
        def one(i, carry):
            rows = pl.ds(pl.multiple_of(i * tile_g, tile_g), tile_g)
            left = act[:, :, rows].reshape(N * Tc, tile_g)
            w2[rows, :] = contract_first(left, dy[...].reshape(N * Tc, Dc)).astype(bf16)
            return carry

        lax.fori_loop(0, H // tile_g, one, 0)

    tile_g = min(256, H)
    gs_copy = pltpu.make_async_copy(w2, gs_out, out_sem.at[0])
    gf_copy = pltpu.make_async_copy(gf_half, gf_out, out_sem.at[1])
    for i in range(q):
        use_piece(c, i)
    act_step(last - 1)
    local[4].wait()
    row_rest(x_ref, x, x_s, x_r)
    gf_block(c, True)

    for k in range(last):
        for j in range(SUB):
            rows_j = pl.ds(j * part, part)
            for side in range(2):
                @pl.when(ag_gets(side, k))
                def _():
                    s = ag_got(side, k)
                    ag_copy(gp, s, rows_j, side, gp_s.at[side, k, j], gp_r.at[side, k, j]).wait_recv()
                    if k + 1 < last:
                        @pl.when(ag_sends(side, k + 1))
                        def _():
                            ag_copy(gp, s, rows_j, side, gp_s.at[side, k + 1, j],
                                    gp_r.at[side, k + 1, j]).start()
            for side in range(2):
                @pl.when(ag_gets(side, k))
                def _():
                    use_piece(ag_got(side, k), j)
        if k + 1 < last:
            for side in range(2):
                s = ag_got(side, k)

                @pl.when(ag_gets(side, k) & (s != far))
                def _():
                    gf_block(s, False)
        if k == 0:
            gs_all()
            gs_copy.start()
    gf_block(far, False, True)
    gf_copy.start()

    for k in range(1, R):
        p = lax.rem(r + k, R)
        row_got(gi_send.at[0, pl.ds(0, Tr)], gi_recv, p, gi_s.at[p], gi_r).wait_recv()

    def total_strip(rows):
        total = gi_recv[0, rows, :].astype(f32)
        for p in range(1, R):
            total = total + gi_recv[p, rows, :].astype(f32)
        gi_out[rows, :] = total.astype(bf16)

    strips(0, Tr, total_strip)

    row_end(0, dy_ref, dy, dy_s, dy_r)
    row_end(1, x_ref, x, x_s, x_r)
    for s in range(N):
        for i in range(q):
            @pl.when(q * s + i != r)
            def _():
                gi_copy(s, i).wait_send()
    for side in range(2):
        for k in range(last):
            @pl.when(ag_sends(side, k))
            def _():
                s = ag_shard(side, k)
                ag_copy(pre, s, None, side, pr_s.at[side, k], pr_r.at[side, k],
                        pre_ref if k == 0 else None).wait_send()
                for j in range(SUB):
                    ag_copy(gp, s, pl.ds(j * part, part), side, gp_s.at[side, k, j],
                            gp_r.at[side, k, j]).wait_send()

        @pl.when(rs_sends(side, last - 1))
        def _():
            for j in range(FINE):
                rs_copy(side, last - 1, j).wait_send()
    for copy in (gs_copy, gf_copy):
        copy.wait()


def exchange(R, N, x, dy, pre, w1, w2):
    Tr, Dc = dy.shape
    Tc, H = pre.shape
    SUB = R // N
    bf16 = jnp.bfloat16
    dma = pltpu.SemaphoreType.DMA
    hbm = pl.BlockSpec(memory_space=pl.ANY)
    return pl.pallas_call(
        functools.partial(kernel, R, N),
        out_shape=[
            jax.ShapeDtypeStruct((Tr, Dc), bf16),
            jax.ShapeDtypeStruct((H, Dc), bf16),
            jax.ShapeDtypeStruct((Dc, H), bf16),
        ],
        in_specs=[hbm] * 5,
        out_specs=[pl.BlockSpec(memory_space=pltpu.VMEM)] + [hbm] * 2,
        scratch_shapes=[
            pltpu.VMEM(w1.shape, bf16),
            pltpu.VMEM(w2.shape, bf16),
            pltpu.VMEM((R, Tr, Dc), bf16),
            pltpu.VMEM((R, Tr, Dc), bf16),
            pltpu.VMEM((N, Tc, H), bf16),
            pltpu.VMEM((N, Tc, H), bf16),
            pltpu.VMEM((N, Tc, H), bf16),
            pltpu.VMEM((N, Tc, H), bf16),
            pltpu.VMEM((Tc, H), jnp.float32),
            pltpu.VMEM((2, N - 1, Tc, H), bf16),
            pltpu.VMEM((N, Tc, Dc), bf16),
            pltpu.VMEM((R, Tr, Dc), bf16),
            pltpu.VMEM((Tc, H), jnp.float32),
            pltpu.VMEM((Dc, H), jnp.float32),
            pltpu.VMEM((Dc, H), bf16),
            dma((5,)),
            dma((2,)),
            dma((R // 2,)), dma((R,)), dma((R // 2,)), dma((R,)), dma((2, R // 2)),
            dma((2, N - 1)), dma((2, N - 1)),
            dma((2, N - 1, 2 * SUB)), dma((2, N - 1, 2 * SUB)),
            dma((2, N - 1, SUB)), dma((2, N - 1, SUB)),
            dma((R,)), dma((R,)),
        ],
        compiler_params=pltpu.CompilerParams(
            collective_id=0, has_side_effects=True, vmem_limit_bytes=60 * 2**20
        ),
    )(x, dy, pre, w1, w2)


def widen(factor, *arrays):
    steps = 8
    specs = [pl.BlockSpec((a.shape[0] // steps, a.shape[1]), lambda i: (i, 0)) for a in arrays]

    def body(a_ref, b_ref, a_out, b_out):
        a_out[...] = a_ref[...].astype(jnp.float32) * factor
        b_out[...] = b_ref[...].astype(jnp.float32) * factor

    return pl.pallas_call(
        body,
        grid=(steps,),
        in_specs=specs,
        out_specs=specs,
        out_shape=[jax.ShapeDtypeStruct(a.shape, jnp.float32) for a in arrays],
        compiler_params=pltpu.CompilerParams(vmem_limit_bytes=60 * 2**20),
    )(*arrays)


def on_device(R, N, inputs_act, out_grad, pre_act, w_first, w_second):
    total_tokens = pre_act.shape[0] * N
    factor = 1.0 / math.sqrt(total_tokens)
    grad_input, gs, gf = exchange(R, N, inputs_act, out_grad, pre_act, w_first, w_second)
    grad_first, grad_second = widen(factor, gf, gs)
    return (grad_input, grad_first, grad_second)


def solution(mesh):
    in_specs = (P("row", "col"), P("row", "col"), P("col", "row"), P("col", "row"), P("row", "col"))
    out_specs = (P("row", "col"), P("col", "row"), P("row", "col"))
    return jax.shard_map(
        functools.partial(on_device, mesh.shape["row"], mesh.shape["col"]),
        mesh=mesh, in_specs=in_specs, out_specs=out_specs, check_vma=False,
    )
```
